256 devices in a mesh: grp: 8 (over y, core), rows: 32 (over z, x).
Axes of the slice: x: 4, y: 4, z: 8, core: 2. Of those that a mesh axis runs over, the one named last changes fastest.
Arguments:
- rhs: float32 [16384, 64, 128], P(('grp', 'rows')), may hold values from -6 to 6
- fine_diag: bfloat16 [16384, 64, 64], P(('grp', 'rows')), may hold values from -0.2 to 1.2
- fine_smoother: bfloat16 [16384, 64, 64], P(('grp', 'rows')), may hold values from -4 to 4
- fine_blocks: bfloat16 [16384, 7, 64, 64], P(('grp', 'rows')), may hold values from -0.1796875 to 0.1796875
- fine_cols: int32 [16384, 7], P(('grp', 'rows')), may hold values from 0 to 16383, as said below
- aggregate: int32 [16384], P(('grp', 'rows')), may hold values from 0 to 2047, as said below
- coarse_diag: bfloat16 [2048, 64, 64], P('rows'), may hold values from -0.8 to 4.8
- coarse_smoother: bfloat16 [2048, 64, 64], P('rows'), may hold values from -1 to 1
- coarse_blocks: bfloat16 [2048, 7, 64, 64], P('rows'), may hold values from -0.71875 to 0.71875
- coarse_cols: int32 [2048, 7], P('rows'), may hold values from 0 to 2047, as said below
Outputs:
- solution: float32 [16384, 64, 128], P(('grp', 'rows'))
The draws below stay inside these ranges and needn't reach their ends.
Inputs may be any that keep to these rules, and one draw needn't show every extreme that they name: fine_cols row i names rows within 32 of i; the distance 32 is reached. coarse_cols row c names rows within 32 of c; the distance 32 is reached. `aggregate`: aggregate_i lies in [r * 64, (r + 1) * 64) with r = (i // 64) mod 32.
All inputs are finite; a program needn't handle non-finite values.
Results may differ from the reference program's by a relative error of at most 0.001.
The reference program's roundings to bfloat16 on the way count: a program that leaves them out, or rounds other values in their place, can miss the bound.
Values may be sent and summed in bfloat16 or wider, within the bound.
No kernel may reach another device: no remote copies, remote signals or barrier semaphores. Data moves between devices by JAX's collectives and lax.ppermute only.
A program may use at most 128 MiB of HBM per device.

```python
import jax
import jax.numpy as jnp
from jax import lax

B = 64
NEIGH = 7
R_DEV = 64
NRHS = 128
C_DEV = 64
NF = 16384
NC = 2048
N_ROWS = 32


def build_blocks(key, count, scale):
    shape = (count, B, B)
    noise = jnp.clip(0.04 * jax.random.normal(key, shape, jnp.float32), -0.16, 0.16)
    return scale * (jnp.eye(B, dtype=jnp.float32)[None] + noise)


def neighbour_columns(key, count, reach, block):
    key_distance, key_direction, key_chosen = jax.random.split(key, 3)
    distance = jax.random.randint(key_distance, (count, NEIGH), 1, reach + 1)
    direction = 2 * jax.random.randint(key_direction, (count, NEIGH), 0, 2) - 1
    offset = distance * direction
    row_ids = jnp.arange(count, dtype=jnp.int32)
    groups = count // block
    chosen = jax.random.randint(key_chosen, (groups, 2), 0, block)
    within = row_ids % block
    owner_block = row_ids // block
    low_hit = within == chosen[owner_block, 0]
    high_hit = within == chosen[owner_block, 1]
    first_slot = jnp.where(high_hit, reach, jnp.where(low_hit, -reach, offset[:, 0]))
    second_slot = jnp.where(row_ids == 0, -reach, jnp.where(row_ids == count - 1, reach, offset[:, 1]))
    offset = jnp.concatenate([first_slot[:, None], second_slot[:, None], offset[:, 2:]], axis=1)
    return jnp.clip(row_ids[:, None] + offset, 0, count - 1).astype(jnp.int32)


def draw_fine_diag(key, part):
    return build_blocks(jax.random.fold_in(key, 11), NF, 1.0).astype(jnp.bfloat16)


def draw_fine_smoother(key, part):
    return jnp.linalg.inv(build_blocks(jax.random.fold_in(key, 11), NF, 1.0)).astype(jnp.bfloat16)


def draw_coarse_diag(key, part):
    return build_blocks(jax.random.fold_in(key, 23), NC, 4.0).astype(jnp.bfloat16)


def draw_coarse_smoother(key, part):
    return jnp.linalg.inv(build_blocks(jax.random.fold_in(key, 23), NC, 4.0)).astype(jnp.bfloat16)


def draw_fine_cols(key, part):
    return neighbour_columns(jax.random.fold_in(key, 37), NF, R_DEV // 2, R_DEV)


def draw_coarse_cols(key, part):
    return neighbour_columns(jax.random.fold_in(key, 41), NC, C_DEV // 2, C_DEV)


def draw_aggregate(key, part):
    row_ids = jnp.arange(NF, dtype=jnp.int32)
    owner_row = row_ids // R_DEV % N_ROWS
    local_slot = jax.random.randint(jax.random.fold_in(key, 53), (NF,), 0, C_DEV)
    local_slot = jnp.where(row_ids == 0, 0, jnp.where(row_ids == NF - 1, C_DEV - 1, local_slot))
    return (owner_row * C_DEV + local_slot).astype(jnp.int32)


def shard_levels(key, extent, cuts, smallest, largest):
    def one(axis_at, parts):
        draws = jax.random.uniform(jax.random.fold_in(jax.random.fold_in(key, 6), axis_at), (parts,), jnp.float32, smallest / len(cuts), largest / len(cuts))
        return jnp.repeat(jnp.exp(draws), extent[axis_at] // parts).reshape((-1,) + (1,) * (len(extent) - axis_at - 1))

    gain = one(*cuts[0])
    for cut in cuts[1:]:
        gain = gain * one(*cut)
    return gain


def centred(key, shape, width, most, cuts=(), kind=jnp.bfloat16):
    entries = jax.random.normal(key, shape, jnp.float32) * width
    if len(cuts) > 0:
        entries = shard_levels(key, shape, cuts, -0.22, 0.18) * entries
    return jnp.clip(entries, min=-most, max=most).astype(kind)


def setup_inputs(seed: int = 0) -> dict:
    seeds = jax.random.split(jax.random.key(seed), 11)
    rhs = centred(seeds[0], (NF, B, NRHS), 1.0, 6.0, ((0, 256),), jnp.float32)
    fine_diag = draw_fine_diag(jax.random.fold_in(seeds[10], 71), 0)
    fine_smoother = draw_fine_smoother(jax.random.fold_in(seeds[10], 71), 0)
    fine_blocks = centred(seeds[3], (NF, NEIGH, B, B), 0.03, 0.1796875, ((0, 256),))
    fine_cols = draw_fine_cols(jax.random.fold_in(seeds[10], 71), 0)
    aggregate = draw_aggregate(jax.random.fold_in(seeds[10], 71), 0)
    coarse_diag = draw_coarse_diag(jax.random.fold_in(seeds[10], 71), 0)
    coarse_smoother = draw_coarse_smoother(jax.random.fold_in(seeds[10], 71), 0)
    coarse_blocks = centred(seeds[8], (NC, NEIGH, B, B), 0.12, 0.71875, ((0, 32),))
    coarse_cols = draw_coarse_cols(jax.random.fold_in(seeds[10], 71), 0)
    return dict(rhs=rhs, fine_diag=fine_diag, fine_smoother=fine_smoother, fine_blocks=fine_blocks, fine_cols=fine_cols, aggregate=aggregate, coarse_diag=coarse_diag, coarse_smoother=coarse_smoother, coarse_blocks=coarse_blocks, coarse_cols=coarse_cols)


damping = 0.8

def rounded(values):
    return lax.optimization_barrier(values.astype(jnp.bfloat16)).astype(jnp.float32)

def block_product(blocks, vector):
    return jnp.einsum('nab,nbk->nak', blocks.astype(jnp.float32), rounded(vector), precision=lax.Precision.HIGHEST)

def apply_operator(diag_blocks, off_blocks, columns, vector, height):
    vector_low = rounded(vector)
    group_count = vector.shape[0] // height

    def one_group(group_index):
        first_row = group_index * height
        diag_part = lax.dynamic_slice_in_dim(diag_blocks, first_row, height, 0).astype(jnp.float32)
        off_part = lax.dynamic_slice_in_dim(off_blocks, first_row, height, 0).astype(jnp.float32)
        column_part = lax.dynamic_slice_in_dim(columns, first_row, height, 0)
        own_rows = lax.dynamic_slice_in_dim(vector_low, first_row, height, 0)
        nearby = jnp.take(vector_low, column_part, axis=0)
        own_term = jnp.einsum('nab,nbk->nak', diag_part, own_rows, precision=lax.Precision.HIGHEST)
        off_term = jnp.einsum('njab,njbk->nak', off_part, nearby, precision=lax.Precision.HIGHEST)
        return own_term + off_term
    result = lax.map(one_group, jnp.arange(group_count, dtype=jnp.int32))
    return result.reshape(vector.shape)

def reference(rhs, fine_diag, fine_smoother, fine_blocks, fine_cols, aggregate, coarse_diag, coarse_smoother, coarse_blocks, coarse_cols):
    first_iterate = damping * block_product(fine_smoother, rhs)
    first_residual = rhs - apply_operator(fine_diag, fine_blocks, fine_cols, first_iterate, R_DEV)
    second_iterate = first_iterate + damping * block_product(fine_smoother, first_residual)
    second_residual = rhs - apply_operator(fine_diag, fine_blocks, fine_cols, second_iterate, R_DEV)
    coarse_rhs = jax.ops.segment_sum(second_residual, aggregate, num_segments=NC)
    coarse_first = damping * block_product(coarse_smoother, coarse_rhs)
    coarse_image = apply_operator(coarse_diag, coarse_blocks, coarse_cols, coarse_first, C_DEV)
    coarse_second = coarse_first + damping * block_product(coarse_smoother, coarse_rhs - coarse_image)
    return second_iterate + jnp.take(coarse_second, aggregate, axis=0)
```

```python
import functools

import jax
import jax.numpy as jnp
from jax import lax
from jax.experimental import pallas as pl
from jax.experimental.pallas import tpu as pltpu
from jax.sharding import PartitionSpec as P

f32, bf16 = jnp.float32, jnp.bfloat16
damping = 0.8
fine_axes = ("grp", "rows")


def dot(a, b):
    return jnp.dot(a, b, preferred_element_type=f32)


def params(mib):
    return pltpu.CompilerParams(vmem_limit_bytes=mib << 20)


def cost(flops, nbytes):
    return pl.CostEstimate(flops=flops, bytes_accessed=nbytes, transcendentals=0)


def row_block(step, *tail):
    return pl.BlockSpec((step,) + tail, lambda i: (i,) + (0,) * len(tail))


vmem = pl.BlockSpec(memory_space=pltpu.VMEM)
smem = pl.BlockSpec(memory_space=pltpu.SMEM)
hbm = pl.BlockSpec(memory_space=pltpu.HBM)


def shape(kind, *dims):
    return jax.ShapeDtypeStruct(dims, kind)


def in_hbm(array):
    return pltpu.with_memory_space_constraint(array, pltpu.HBM)


def first_kernel(step, smoother, rhs, low, high, smoother_here, rhs_here, sem):
    n, half = rhs.shape[0], low.shape[0]
    copies = []
    for s in range(0, n, step):
        rows = slice(s, s + step)
        k = 2 * (s // step)
        pair = (
            pltpu.make_async_copy(smoother.at[rows], smoother_here.at[rows], sem.at[k]),
            pltpu.make_async_copy(rhs.at[rows], rhs_here.at[rows], sem.at[k + 1]),
        )
        for c in pair:
            c.start()
        copies.append(pair)
    for s in range(0, n, step):
        for c in copies[s // step]:
            c.wait()
        products = [dot(smoother_here[r], rhs_here[r].astype(bf16)) for r in range(s, s + step)]
        for r in range(s, s + step):
            out = low if r < half else high
            out[r % half] = (damping * products[r - s]).astype(bf16)


def first_iterate(smoother, rhs):
    n, b, k = rhs.shape
    step = 16
    return pl.pallas_call(
        functools.partial(first_kernel, step),
        in_specs=[hbm, hbm],
        out_specs=[vmem, vmem],
        out_shape=[shape(bf16, n // 2, b, k)] * 2,
        scratch_shapes=[
            pltpu.VMEM((n, b, b), bf16),
            pltpu.VMEM((n, b, k), f32),
            pltpu.SemaphoreType.DMA((2 * n // step,)),
        ],
        compiler_params=params(16),
        cost_estimate=cost(2 * n * b * b * k, 6 * n * b * k + 4 * n * b * b),
        name="first_iterate",
    )(in_hbm(smoother), in_hbm(rhs))


def pack_kernel(step, off, diag, out):
    for r in range(step):
        out[r] = jnp.concatenate([off[r, j] for j in range(off.shape[1])] + [diag[r]], axis=1)


def packed(off, diag):
    rows, near, b, _ = off.shape
    step = 16
    return pl.pallas_call(
        functools.partial(pack_kernel, step),
        grid=(rows // step,),
        in_specs=[row_block(step, near, b, b), row_block(step, b, b)],
        out_specs=row_block(step, b, (near + 1) * b),
        out_shape=shape(bf16, rows, b, (near + 1) * b),
        compiler_params=params(16),
        cost_estimate=cost(0, 6 * rows * b * b * (near + 1)),
        name="packed",
    )(in_hbm(off), in_hbm(diag))


def load_extended(extended, *parts):
    at = 0
    for part in parts:
        extended[at : at + part.shape[0]] = part[...]
        at += part.shape[0]


def images(step, s, cols, base, skip, own, blocks, extended):
    out = []
    for r in range(step):
        i = s * step + r
        vector = [extended[cols[j, skip + i] - base] for j in range(cols.shape[0])]
        vector.append(extended[own + i])
        out.append(dot(blocks[skip + i], jnp.concatenate(vector, axis=0)))
    return out


def fine_start(height):
    return (lax.axis_index("grp") * lax.axis_size("rows") + lax.axis_index("rows")) * height


def kept_side():
    return (lax.axis_index("grp") + lax.axis_index("rows")) & 1


def second_kernel(
    step, upper, cols, first_part, middle, last_part, blocks, smoother, rhs, out, out_low, extended
):
    half = out.shape[0]
    load_extended(extended, first_part, middle, last_part)
    skip = half if upper else 0
    base = fine_start(rhs.shape[0]) + skip - half

    @pl.loop(0, half // step)
    def _(s):
        image = images(step, s, cols, base, skip, half, blocks, extended)
        rows = [s * step + r for r in range(step)]
        right = [rhs[skip + i] for i in rows]
        first = [dot(smoother[skip + i], right[r].astype(bf16)) for r, i in enumerate(rows)]
        residual = [(right[r] - image[r]).astype(bf16) for r in range(step)]
        products = [dot(smoother[skip + i], residual[r]) for r, i in enumerate(rows)]
        for r, i in enumerate(rows):
            second = damping * first[r] + damping * products[r]
            out[i] = second
            out_low[i] = second.astype(bf16)


def second_iterate(upper, cols, parts, blocks, smoother, rhs):
    n, b, k = rhs.shape
    near, half, step = cols.shape[0], n // 2, 16
    return pl.pallas_call(
        functools.partial(second_kernel, step, upper),
        in_specs=[smem] + [vmem] * 6,
        out_specs=[vmem] * 2,
        out_shape=[shape(f32, half, b, k), shape(bf16, half, b, k)],
        scratch_shapes=[pltpu.VMEM((3 * half, b, k), bf16)],
        compiler_params=params(12),
        cost_estimate=cost(n * b * b * k * (near + 3), n * b * b * (near + 2) + 7 * n * b * k),
        name="second_upper" if upper else "second_lower",
    )(cols, *parts, blocks, smoother, rhs)


def restrict_kernel(step, upper, cols, aggregate, first_part, middle, last_part, blocks, rhs, *rest):
    before, (total, extended) = rest[:-2], rest[-2:]
    half, coarse = middle.shape[0], total.shape[0]
    load_extended(extended, first_part, middle, last_part)
    if not before:
        total[...] = jnp.zeros_like(total)
    skip = half if upper else 0
    base = fine_start(rhs.shape[0]) + skip - half
    turn = kept_side() * (coarse // 2) - lax.axis_index("rows") * coarse + coarse

    @pl.loop(0, half // step)
    def _(s):
        image = images(step, s, cols, base, skip, half, blocks, extended)
        residual = [rhs[skip + s * step + r] - image[r] for r in range(step)]
        for r in range(step):
            slot = lax.rem(aggregate[skip + s * step + r] + turn, coarse)
            total[slot] = total[slot] + residual[r]


def restricted(upper, cols, aggregate, parts, blocks, rhs, coarse, *before):
    n, b, k = rhs.shape
    near, half, step = cols.shape[0], n // 2, 16
    return pl.pallas_call(
        functools.partial(restrict_kernel, step, upper),
        in_specs=[smem, smem] + [vmem] * (5 + len(before)),
        out_specs=vmem,
        out_shape=shape(f32, coarse, b, k),
        scratch_shapes=[pltpu.VMEM((3 * half, b, k), bf16)],
        input_output_aliases={7: 0} if before else {},
        compiler_params=params(12),
        cost_estimate=cost(n * b * b * k * (near + 1), n * b * b * (near + 1) + 6 * n * b * k),
        name="restrict_upper" if upper else "restrict_lower",
    )(cols, aggregate, *parts, blocks, rhs, *before)


def coarse_first_kernel(upper, lower, more_upper, more_lower, smoother, rhs, first):
    quarter = upper.shape[0]
    skip = kept_side() * 2 * quarter
    for total, more, at in ((upper, more_upper, 0), (lower, more_lower, quarter)):
        full = [total[r] + more[r].astype(f32) for r in range(quarter)]
        products = [dot(smoother[skip + at + r], full[r].astype(bf16)) for r in range(quarter)]
        for r in range(quarter):
            rhs[at + r] = full[r]
            first[at + r] = (damping * products[r]).astype(bf16)


def coarse_first(upper, lower, more_upper, more_lower, smoother):
    n, b, k = 2 * upper.shape[0], upper.shape[1], upper.shape[2]
    return pl.pallas_call(
        coarse_first_kernel,
        in_specs=[vmem] * 5,
        out_specs=[vmem] * 2,
        out_shape=[shape(f32, n, b, k), shape(bf16, n, b, k)],
        compiler_params=params(16),
        cost_estimate=cost(2 * n * b * b * k, 12 * n * b * k + 4 * n * b * b),
        name="coarse_first",
    )(upper, lower, more_upper, more_lower, smoother)


def coarse_second_kernel(
    step, cols, halo, own, other, blocks, smoother, rhs, out, extended
):
    n = own.shape[0]
    skip = kept_side() * n
    base = lax.axis_index("rows") * 2 * n + skip - n
    at = 2 * skip
    extended[pl.ds(at, n)] = halo[...]
    extended[n : 2 * n] = own[...]
    extended[pl.ds(2 * n - at, n)] = other[...]

    @pl.loop(0, n // step)
    def _(s):
        image = images(step, s, cols, base, skip, n, blocks, extended)
        rows = [s * step + r for r in range(step)]
        first = [damping * dot(smoother[skip + i], rhs[i].astype(bf16)) for i in rows]
        residual = [(rhs[i] - image[r]).astype(bf16) for r, i in enumerate(rows)]
        products = [dot(smoother[skip + i], residual[r]) for r, i in enumerate(rows)]
        for r, i in enumerate(rows):
            out[i] = first[r] + damping * products[r]


def coarse_second(cols, halo, own, other, blocks, smoother, rhs):
    n, b, k = rhs.shape
    near, step = cols.shape[0], 16
    return pl.pallas_call(
        functools.partial(coarse_second_kernel, step),
        in_specs=[smem] + [vmem] * 6,
        out_specs=vmem,
        out_shape=shape(f32, n, b, k),
        scratch_shapes=[pltpu.VMEM((3 * n, b, k), bf16)],
        compiler_params=params(12),
        cost_estimate=cost(2 * n * b * b * k * (near + 3), 2 * n * b * b * (near + 2) + 14 * n * b * k),
        name="coarse_second",
    )(cols, halo, own, other, blocks, smoother, rhs)


def correct_kernel(aggregate, lower, upper, kept, given, out, table, staged, sem):
    half, n = kept.shape[0], staged.shape[0]
    turn = kept_side() * half - lax.axis_index("rows") * 2 * half + 2 * half
    table[0:half] = kept[...]
    table[half : 2 * half] = given[...]
    copies = []
    for s in range(sem.shape[0]):
        step = n // sem.shape[0]
        for r in range(s * step, (s + 1) * step):
            fine = lower[r] if r < n // 2 else upper[r - n // 2]
            staged[r] = fine + table[lax.rem(aggregate[r] + turn, 2 * half)]
        rows = slice(s * step, (s + 1) * step)
        copies.append(pltpu.make_async_copy(staged.at[rows], out.at[rows], sem.at[s]))
        copies[-1].start()
    for c in copies:
        c.wait()


def corrected(aggregate, lower, upper, kept, given):
    n, b, k = aggregate.shape[0], lower.shape[1], lower.shape[2]
    return pl.pallas_call(
        correct_kernel,
        in_specs=[smem] + [vmem] * 4,
        out_specs=hbm,
        out_shape=shape(f32, n, b, k),
        scratch_shapes=[
            pltpu.VMEM((2 * kept.shape[0], b, k), f32),
            pltpu.VMEM((n, b, k), f32),
            pltpu.SemaphoreType.DMA((4,)),
        ],
        compiler_params=params(16),
        cost_estimate=cost(n * b * k, 12 * n * b * k),
        name="corrected",
    )(aggregate, lower, upper, kept, given)


def on_device(
    rhs,
    fine_diag,
    fine_smoother,
    fine_blocks,
    fine_cols,
    aggregate,
    coarse_diag,
    coarse_smoother,
    coarse_blocks,
    coarse_cols,
):
    grp, rows = lax.axis_size("grp"), lax.axis_size("rows")
    coarse = coarse_diag.shape[0]
    half = coarse // 2
    fine_cols, coarse_cols = fine_cols.T, coarse_cols.T
    ends = range(grp * rows - 1)
    to_next = lambda v: lax.ppermute(v, fine_axes, [(i, i + 1) for i in ends])
    to_previous = lambda v: lax.ppermute(v, fine_axes, [(i + 1, i) for i in ends])

    low, high = first_iterate(fine_smoother, rhs)
    before, after = to_next(high), to_previous(low)
    fine = packed(fine_blocks, fine_diag)
    lower, low2 = second_iterate(False, fine_cols, (before, low, high), fine, fine_smoother, rhs)
    after2 = to_previous(low2)
    upper, high2 = second_iterate(True, fine_cols, (low, high, after), fine, fine_smoother, rhs)
    before2 = to_next(high2)
    after2, blocks = lax.optimization_barrier((after2, packed(coarse_blocks, coarse_diag)))
    total = restricted(True, fine_cols, aggregate, (low2, high2, after2), fine, rhs, coarse)
    total = restricted(False, fine_cols, aggregate, (before2, low2, high2), fine, rhs, coarse, total)
    kept, given = total[:half], total[half:]

    across = [(i, i ^ 1) for i in range(grp)]
    near = [(i, i ^ 2) for i in range(grp)]
    far = [(i, i ^ 6) for i in range(grp)]
    total = kept + lax.ppermute(given, "grp", across)
    quarter = half // 2
    one, two = total[:quarter], total[quarter:]
    from_one = lax.ppermute(one.astype(bf16), "grp", near)
    from_two = lax.ppermute(two.astype(bf16), "grp", far)
    one, two = one + from_one.astype(f32), two + from_two.astype(f32)
    from_one = lax.ppermute(one.astype(bf16), "grp", far)
    from_two = lax.ppermute(two.astype(bf16), "grp", near)

    coarse_rhs, rounded_first = coarse_first(one, two, from_one, from_two, coarse_smoother)
    towards = []
    for i in range(grp):
        for r in range(rows):
            source = r - 1 if (i + r) % 2 == 0 else r + 1
            if 0 <= source < rows:
                towards.append((i * rows + source, i * rows + r))
    other = lax.ppermute(rounded_first, "grp", across)
    halo = lax.ppermute(rounded_first, fine_axes, towards)
    mine = coarse_second(
        coarse_cols,
        halo,
        rounded_first,
        other,
        blocks,
        coarse_smoother,
        coarse_rhs,
    )
    theirs = lax.ppermute(mine, "grp", across)
    return corrected(aggregate, lower, upper, mine, theirs)


def solution(mesh):
    in_specs = (
        P(("grp", "rows"), None, None),
        P(("grp", "rows"), None, None),
        P(("grp", "rows"), None, None),
        P(("grp", "rows"), None, None, None),
        P(("grp", "rows"), None),
        P(("grp", "rows")),
        P("rows", None, None),
        P("rows", None, None),
        P("rows", None, None, None),
        P("rows", None),
    )
    out_specs = P(("grp", "rows"), None, None)
    return jax.shard_map(
        on_device, mesh=mesh, in_specs=in_specs, out_specs=out_specs, check_vma=False
    )
```

```python
import functools

import jax
import jax.numpy as jnp
from jax import lax
from jax.experimental import pallas as pl
from jax.experimental.pallas import tpu as pltpu
from jax.sharding import PartitionSpec as P

f32, bf16 = jnp.float32, jnp.bfloat16
damping = 0.8
fine_axes = ("grp", "rows")


def dot(a, b):
    return jnp.dot(a, b, preferred_element_type=f32)


def params(mib):
    return pltpu.CompilerParams(vmem_limit_bytes=mib << 20)


def cost(flops, nbytes):
    return pl.CostEstimate(flops=flops, bytes_accessed=nbytes, transcendentals=0)


def row_block(step, *tail):
    return pl.BlockSpec((step,) + tail, lambda i: (i,) + (0,) * len(tail))


vmem = pl.BlockSpec(memory_space=pltpu.VMEM)
smem = pl.BlockSpec(memory_space=pltpu.SMEM)
hbm = pl.BlockSpec(memory_space=pltpu.HBM)


def shape(kind, *dims):
    return jax.ShapeDtypeStruct(dims, kind)


def in_hbm(array):
    return pltpu.with_memory_space_constraint(array, pltpu.HBM)


def first_kernel(step, smoother, rhs, low, high, smoother_here, rhs_here, sem):
    n, half = rhs.shape[0], low.shape[0]
    copies = []
    for s in range(0, n, step):
        rows = slice(s, s + step)
        k = 2 * (s // step)
        pair = (
            pltpu.make_async_copy(smoother.at[rows], smoother_here.at[rows], sem.at[k]),
            pltpu.make_async_copy(rhs.at[rows], rhs_here.at[rows], sem.at[k + 1]),
        )
        for c in pair:
            c.start()
        copies.append(pair)
    for s in range(0, n, step):
        for c in copies[s // step]:
            c.wait()
        products = [dot(smoother_here[r], rhs_here[r].astype(bf16)) for r in range(s, s + step)]
        for r in range(s, s + step):
            out = low if r < half else high
            out[r % half] = (damping * products[r - s]).astype(bf16)


def first_iterate(smoother, rhs):
    n, b, k = rhs.shape
    step = 16
    return pl.pallas_call(
        functools.partial(first_kernel, step),
        in_specs=[hbm, hbm],
        out_specs=[vmem, vmem],
        out_shape=[shape(bf16, n // 2, b, k)] * 2,
        scratch_shapes=[
            pltpu.VMEM((n, b, b), bf16),
            pltpu.VMEM((n, b, k), f32),
            pltpu.SemaphoreType.DMA((2 * n // step,)),
        ],
        compiler_params=params(16),
        cost_estimate=cost(2 * n * b * b * k, 6 * n * b * k + 4 * n * b * b),
        name="first_iterate",
    )(in_hbm(smoother), in_hbm(rhs))


def pack_kernel(step, off, diag, out):
    for r in range(step):
        out[r] = jnp.concatenate([off[r, j] for j in range(off.shape[1])] + [diag[r]], axis=1)


def packed(off, diag):
    rows, near, b, _ = off.shape
    step = 16
    return pl.pallas_call(
        functools.partial(pack_kernel, step),
        grid=(rows // step,),
        in_specs=[row_block(step, near, b, b), row_block(step, b, b)],
        out_specs=row_block(step, b, (near + 1) * b),
        out_shape=shape(bf16, rows, b, (near + 1) * b),
        compiler_params=params(16),
        cost_estimate=cost(0, 6 * rows * b * b * (near + 1)),
        name="packed",
    )(in_hbm(off), in_hbm(diag))


def load_extended(extended, *parts):
    at = 0
    for part in parts:
        extended[at : at + part.shape[0]] = part[...]
        at += part.shape[0]


def images(step, s, cols, base, skip, own, blocks, extended):
    out = []
    for r in range(step):
        i = s * step + r
        vector = [extended[cols[j, skip + i] - base] for j in range(cols.shape[0])]
        vector.append(extended[own + i])
        out.append(dot(blocks[skip + i], jnp.concatenate(vector, axis=0)))
    return out


def fine_start(height):
    return (lax.axis_index("grp") * lax.axis_size("rows") + lax.axis_index("rows")) * height


def kept_side():
    return (lax.axis_index("grp") + lax.axis_index("rows")) & 1


def second_kernel(
    step, upper, cols, first_part, middle, last_part, blocks, smoother, rhs, out, out_low, extended
):
    half = out.shape[0]
    load_extended(extended, first_part, middle, last_part)
    skip = half if upper else 0
    base = fine_start(rhs.shape[0]) + skip - half

    @pl.loop(0, half // step)
    def _(s):
        image = images(step, s, cols, base, skip, half, blocks, extended)
        rows = [s * step + r for r in range(step)]
        right = [rhs[skip + i] for i in rows]
        first = [dot(smoother[skip + i], right[r].astype(bf16)) for r, i in enumerate(rows)]
        residual = [(right[r] - image[r]).astype(bf16) for r in range(step)]
        products = [dot(smoother[skip + i], residual[r]) for r, i in enumerate(rows)]
        for r, i in enumerate(rows):
            second = damping * first[r] + damping * products[r]
            out[i] = second
            out_low[i] = second.astype(bf16)


def second_iterate(upper, cols, parts, blocks, smoother, rhs):
    n, b, k = rhs.shape
    near, half, step = cols.shape[0], n // 2, 16
    return pl.pallas_call(
        functools.partial(second_kernel, step, upper),
        in_specs=[smem] + [vmem] * 6,
        out_specs=[vmem] * 2,
        out_shape=[shape(f32, half, b, k), shape(bf16, half, b, k)],
        scratch_shapes=[pltpu.VMEM((3 * half, b, k), bf16)],
        compiler_params=params(12),
        cost_estimate=cost(n * b * b * k * (near + 3), n * b * b * (near + 2) + 7 * n * b * k),
        name="second_upper" if upper else "second_lower",
    )(cols, *parts, blocks, smoother, rhs)


def restrict_kernel(step, upper, cols, aggregate, first_part, middle, last_part, blocks, rhs, *rest):
    before, (total, extended) = rest[:-2], rest[-2:]
    half, coarse = middle.shape[0], total.shape[0]
    load_extended(extended, first_part, middle, last_part)
    if not before:
        total[...] = jnp.zeros_like(total)
    skip = half if upper else 0
    base = fine_start(rhs.shape[0]) + skip - half
    turn = kept_side() * (coarse // 2) - lax.axis_index("rows") * coarse + coarse

    @pl.loop(0, half // step)
    def _(s):
        image = images(step, s, cols, base, skip, half, blocks, extended)
        residual = [rhs[skip + s * step + r] - image[r] for r in range(step)]
        for r in range(step):
            slot = lax.rem(aggregate[skip + s * step + r] + turn, coarse)
            total[slot] = total[slot] + residual[r]


def restricted(upper, cols, aggregate, parts, blocks, rhs, coarse, *before):
    n, b, k = rhs.shape
    near, half, step = cols.shape[0], n // 2, 16
    return pl.pallas_call(
        functools.partial(restrict_kernel, step, upper),
        in_specs=[smem, smem] + [vmem] * (5 + len(before)),
        out_specs=vmem,
        out_shape=shape(f32, coarse, b, k),
        scratch_shapes=[pltpu.VMEM((3 * half, b, k), bf16)],
        input_output_aliases={7: 0} if before else {},
        compiler_params=params(12),
        cost_estimate=cost(n * b * b * k * (near + 1), n * b * b * (near + 1) + 6 * n * b * k),
        name="restrict_upper" if upper else "restrict_lower",
    )(cols, aggregate, *parts, blocks, rhs, *before)


def coarse_first_kernel(upper, lower, more_upper, more_lower, smoother, rhs, first):
    quarter = upper.shape[0]
    skip = kept_side() * 2 * quarter
    for total, more, at in ((upper, more_upper, 0), (lower, more_lower, quarter)):
        full = [total[r] + more[r].astype(f32) for r in range(quarter)]
        products = [dot(smoother[skip + at + r], full[r].astype(bf16)) for r in range(quarter)]
        for r in range(quarter):
            rhs[at + r] = full[r]
            first[at + r] = (damping * products[r]).astype(bf16)


def coarse_first(upper, lower, more_upper, more_lower, smoother):
    n, b, k = 2 * upper.shape[0], upper.shape[1], upper.shape[2]
    return pl.pallas_call(
        coarse_first_kernel,
        in_specs=[vmem] * 5,
        out_specs=[vmem] * 2,
        out_shape=[shape(f32, n, b, k), shape(bf16, n, b, k)],
        compiler_params=params(16),
        cost_estimate=cost(2 * n * b * b * k, 12 * n * b * k + 4 * n * b * b),
        name="coarse_first",
    )(upper, lower, more_upper, more_lower, smoother)


def coarse_second_kernel(
    step, cols, halo, own, other, blocks, smoother, rhs, out, extended
):
    n = own.shape[0]
    skip = kept_side() * n
    base = lax.axis_index("rows") * 2 * n + skip - n
    at = 2 * skip
    extended[pl.ds(at, n)] = halo[...]
    extended[n : 2 * n] = own[...]
    extended[pl.ds(2 * n - at, n)] = other[...]

    @pl.loop(0, n // step)
    def _(s):
        image = images(step, s, cols, base, skip, n, blocks, extended)
        rows = [s * step + r for r in range(step)]
        first = [damping * dot(smoother[skip + i], rhs[i].astype(bf16)) for i in rows]
        residual = [(rhs[i] - image[r]).astype(bf16) for r, i in enumerate(rows)]
        products = [dot(smoother[skip + i], residual[r]) for r, i in enumerate(rows)]
        for r, i in enumerate(rows):
            out[i] = first[r] + damping * products[r]


def coarse_second(cols, halo, own, other, blocks, smoother, rhs):
    n, b, k = rhs.shape
    near, step = cols.shape[0], 16
    return pl.pallas_call(
        functools.partial(coarse_second_kernel, step),
        in_specs=[smem] + [vmem] * 6,
        out_specs=vmem,
        out_shape=shape(f32, n, b, k),
        scratch_shapes=[pltpu.VMEM((3 * n, b, k), bf16)],
        compiler_params=params(12),
        cost_estimate=cost(2 * n * b * b * k * (near + 3), 2 * n * b * b * (near + 2) + 14 * n * b * k),
        name="coarse_second",
    )(cols, halo, own, other, blocks, smoother, rhs)


def correct_kernel(aggregate, lower, upper, kept, given, out, staged, sem):
    half, n = kept.shape[0], staged.shape[0]
    turn = kept_side() * half - lax.axis_index("rows") * 2 * half + 2 * half
    copies = []
    for s in range(sem.shape[0]):
        step = n // sem.shape[0]
        for r in range(s * step, (s + 1) * step):
            fine = lower[r] if r < n // 2 else upper[r - n // 2]
            slot = lax.rem(aggregate[r] + turn, 2 * half)
            row = lax.rem(slot, half)
            staged[r] = fine + jnp.where(slot < half, kept[row], given[row])
        rows = slice(s * step, (s + 1) * step)
        copies.append(pltpu.make_async_copy(staged.at[rows], out.at[rows], sem.at[s]))
        copies[-1].start()
    for c in copies:
        c.wait()


def corrected(aggregate, lower, upper, kept, given):
    n, b, k = aggregate.shape[0], lower.shape[1], lower.shape[2]
    return pl.pallas_call(
        correct_kernel,
        in_specs=[smem] + [vmem] * 4,
        out_specs=hbm,
        out_shape=shape(f32, n, b, k),
        scratch_shapes=[
            pltpu.VMEM((n, b, k), f32),
            pltpu.SemaphoreType.DMA((4,)),
        ],
        compiler_params=params(16),
        cost_estimate=cost(n * b * k, 12 * n * b * k),
        name="corrected",
    )(aggregate, lower, upper, kept, given)


def on_device(
    rhs,
    fine_diag,
    fine_smoother,
    fine_blocks,
    fine_cols,
    aggregate,
    coarse_diag,
    coarse_smoother,
    coarse_blocks,
    coarse_cols,
):
    grp, rows = lax.axis_size("grp"), lax.axis_size("rows")
    coarse = coarse_diag.shape[0]
    half = coarse // 2
    fine_cols, coarse_cols = fine_cols.T, coarse_cols.T
    ends = range(grp * rows - 1)
    to_next = lambda v: lax.ppermute(v, fine_axes, [(i, i + 1) for i in ends])
    to_previous = lambda v: lax.ppermute(v, fine_axes, [(i + 1, i) for i in ends])

    low, high = first_iterate(fine_smoother, rhs)
    before, after = to_next(high), to_previous(low)
    fine = packed(fine_blocks, fine_diag)
    lower, low2 = second_iterate(False, fine_cols, (before, low, high), fine, fine_smoother, rhs)
    after2 = to_previous(low2)
    upper, high2 = second_iterate(True, fine_cols, (low, high, after), fine, fine_smoother, rhs)
    before2 = to_next(high2)
    total = restricted(True, fine_cols, aggregate, (low2, high2, after2), fine, rhs, coarse)
    total = restricted(False, fine_cols, aggregate, (before2, low2, high2), fine, rhs, coarse, total)
    kept, given = total[:half], total[half:]

    across = [(i, i ^ 1) for i in range(grp)]
    near = [(i, i ^ 2) for i in range(grp)]
    far = [(i, i ^ 6) for i in range(grp)]
    total = kept + lax.ppermute(given, "grp", across)
    quarter = half // 2
    one, two = total[:quarter], total[quarter:]
    from_one = lax.ppermute(one.astype(bf16), "grp", near)
    from_two = lax.ppermute(two.astype(bf16), "grp", far)
    one, two = one + from_one.astype(f32), two + from_two.astype(f32)
    from_one = lax.ppermute(one.astype(bf16), "grp", far)
    from_two = lax.ppermute(two.astype(bf16), "grp", near)

    coarse_rhs, rounded_first = coarse_first(one, two, from_one, from_two, coarse_smoother)
    towards = []
    for i in range(grp):
        for r in range(rows):
            source = r - 1 if (i + r) % 2 == 0 else r + 1
            if 0 <= source < rows:
                towards.append((i * rows + source, i * rows + r))
    halo = lax.ppermute(rounded_first, fine_axes, towards)
    own, blocks = lax.optimization_barrier((rounded_first, packed(coarse_blocks, coarse_diag)))
    other = lax.ppermute(own, "grp", across)
    mine = coarse_second(
        coarse_cols,
        halo,
        rounded_first,
        other,
        blocks,
        coarse_smoother,
        coarse_rhs,
    )
    theirs = lax.ppermute(mine, "grp", across)
    return corrected(aggregate, lower, upper, mine, theirs)


def solution(mesh):
    in_specs = (
        P(("grp", "rows"), None, None),
        P(("grp", "rows"), None, None),
        P(("grp", "rows"), None, None),
        P(("grp", "rows"), None, None, None),
        P(("grp", "rows"), None),
        P(("grp", "rows")),
        P("rows", None, None),
        P("rows", None, None),
        P("rows", None, None, None),
        P("rows", None),
    )
    out_specs = P(("grp", "rows"), None, None)
    return jax.shard_map(
        on_device, mesh=mesh, in_specs=in_specs, out_specs=out_specs, check_vma=False
    )
```

```python
import functools

import jax
import jax.numpy as jnp
from jax import lax
from jax.experimental import pallas as pl
from jax.experimental.pallas import tpu as pltpu
from jax.sharding import PartitionSpec as P

f32, bf16 = jnp.float32, jnp.bfloat16
damping = 0.8
fine_axes = ("grp", "rows")


def dot(a, b):
    return jnp.dot(a, b, preferred_element_type=f32)


def params(mib):
    return pltpu.CompilerParams(vmem_limit_bytes=mib << 20)


def cost(flops, nbytes):
    return pl.CostEstimate(flops=flops, bytes_accessed=nbytes, transcendentals=0)


def row_block(step, *tail):
    return pl.BlockSpec((step,) + tail, lambda i: (i,) + (0,) * len(tail))


vmem = pl.BlockSpec(memory_space=pltpu.VMEM)
smem = pl.BlockSpec(memory_space=pltpu.SMEM)
hbm = pl.BlockSpec(memory_space=pltpu.HBM)


def shape(kind, *dims):
    return jax.ShapeDtypeStruct(dims, kind)


def in_hbm(array):
    return pltpu.with_memory_space_constraint(array, pltpu.HBM)


def first_kernel(step, start, smoother, rhs, out, smoother_here, rhs_here, sem):
    n = out.shape[0]
    copies = []
    for s in range(0, n, step):
        here, there = slice(s, s + step), slice(start + s, start + s + step)
        k = 2 * (s // step)
        pair = (
            pltpu.make_async_copy(smoother.at[there], smoother_here.at[here], sem.at[k]),
            pltpu.make_async_copy(rhs.at[there], rhs_here.at[here], sem.at[k + 1]),
        )
        for c in pair:
            c.start()
        copies.append(pair)
    for s in range(0, n, step):
        for c in copies[s // step]:
            c.wait()
        products = [dot(smoother_here[r], rhs_here[r].astype(bf16)) for r in range(s, s + step)]
        for r in range(s, s + step):
            out[r] = (damping * products[r - s]).astype(bf16)


def first_iterate(upper, smoother, rhs):
    n, b, k = rhs.shape
    half, step = n // 2, 16
    return pl.pallas_call(
        functools.partial(first_kernel, step, half if upper else 0),
        in_specs=[hbm, hbm],
        out_specs=vmem,
        out_shape=shape(bf16, half, b, k),
        scratch_shapes=[
            pltpu.VMEM((half, b, b), bf16),
            pltpu.VMEM((half, b, k), f32),
            pltpu.SemaphoreType.DMA((2 * half // step,)),
        ],
        compiler_params=params(16),
        cost_estimate=cost(n * b * b * k, 3 * n * b * k + 2 * n * b * b),
        name="first_upper" if upper else "first_lower",
    )(in_hbm(smoother), in_hbm(rhs))


def pack_kernel(step, off, diag, out):
    for r in range(step):
        out[r] = jnp.concatenate([off[r, j] for j in range(off.shape[1])] + [diag[r]], axis=1)


def packed(off, diag):
    rows, near, b, _ = off.shape
    step = 16
    return pl.pallas_call(
        functools.partial(pack_kernel, step),
        grid=(rows // step,),
        in_specs=[row_block(step, near, b, b), row_block(step, b, b)],
        out_specs=row_block(step, b, (near + 1) * b),
        out_shape=shape(bf16, rows, b, (near + 1) * b),
        compiler_params=params(16),
        cost_estimate=cost(0, 6 * rows * b * b * (near + 1)),
        name="packed",
    )(in_hbm(off), in_hbm(diag))


def load_extended(extended, *parts):
    at = 0
    for part in parts:
        extended[at : at + part.shape[0]] = part[...]
        at += part.shape[0]


def images(step, s, cols, base, skip, own, blocks, extended):
    out = []
    for r in range(step):
        i = s * step + r
        vector = [extended[cols[j, skip + i] - base] for j in range(cols.shape[0])]
        vector.append(extended[own + i])
        out.append(dot(blocks[skip + i], jnp.concatenate(vector, axis=0)))
    return out


def fine_start(height):
    return (lax.axis_index("grp") * lax.axis_size("rows") + lax.axis_index("rows")) * height


def kept_side():
    return (lax.axis_index("grp") + lax.axis_index("rows")) & 1


def second_kernel(
    step, upper, cols, first_part, middle, last_part, blocks, smoother, rhs, out, out_low, extended
):
    half = out.shape[0]
    load_extended(extended, first_part, middle, last_part)
    skip = half if upper else 0
    base = fine_start(rhs.shape[0]) + skip - half

    @pl.loop(0, half // step)
    def _(s):
        image = images(step, s, cols, base, skip, half, blocks, extended)
        rows = [s * step + r for r in range(step)]
        right = [rhs[skip + i] for i in rows]
        first = [dot(smoother[skip + i], right[r].astype(bf16)) for r, i in enumerate(rows)]
        residual = [(right[r] - image[r]).astype(bf16) for r in range(step)]
        products = [dot(smoother[skip + i], residual[r]) for r, i in enumerate(rows)]
        for r, i in enumerate(rows):
            second = damping * first[r] + damping * products[r]
            out[i] = second
            out_low[i] = second.astype(bf16)


def second_iterate(upper, cols, parts, blocks, smoother, rhs):
    n, b, k = rhs.shape
    near, half, step = cols.shape[0], n // 2, 16
    return pl.pallas_call(
        functools.partial(second_kernel, step, upper),
        in_specs=[smem] + [vmem] * 6,
        out_specs=[vmem] * 2,
        out_shape=[shape(f32, half, b, k), shape(bf16, half, b, k)],
        scratch_shapes=[pltpu.VMEM((3 * half, b, k), bf16)],
        compiler_params=params(12),
        cost_estimate=cost(n * b * b * k * (near + 3), n * b * b * (near + 2) + 7 * n * b * k),
        name="second_upper" if upper else "second_lower",
    )(cols, *parts, blocks, smoother, rhs)


def restrict_kernel(step, upper, cols, aggregate, first_part, middle, last_part, blocks, rhs, *rest):
    before, (total, extended) = rest[:-2], rest[-2:]
    half, coarse = middle.shape[0], total.shape[0]
    load_extended(extended, first_part, middle, last_part)
    if not before:
        total[...] = jnp.zeros_like(total)
    skip = half if upper else 0
    base = fine_start(rhs.shape[0]) + skip - half
    turn = kept_side() * (coarse // 2) - lax.axis_index("rows") * coarse + coarse

    @pl.loop(0, half // step)
    def _(s):
        image = images(step, s, cols, base, skip, half, blocks, extended)
        residual = [rhs[skip + s * step + r] - image[r] for r in range(step)]
        for r in range(step):
            slot = lax.rem(aggregate[skip + s * step + r] + turn, coarse)
            total[slot] = total[slot] + residual[r]


def restricted(upper, cols, aggregate, parts, blocks, rhs, coarse, *before):
    n, b, k = rhs.shape
    near, half, step = cols.shape[0], n // 2, 16
    return pl.pallas_call(
        functools.partial(restrict_kernel, step, upper),
        in_specs=[smem, smem] + [vmem] * (5 + len(before)),
        out_specs=vmem,
        out_shape=shape(f32, coarse, b, k),
        scratch_shapes=[pltpu.VMEM((3 * half, b, k), bf16)],
        input_output_aliases={7: 0} if before else {},
        compiler_params=params(12),
        cost_estimate=cost(n * b * b * k * (near + 1), n * b * b * (near + 1) + 6 * n * b * k),
        name="restrict_upper" if upper else "restrict_lower",
    )(cols, aggregate, *parts, blocks, rhs, *before)


def coarse_first_kernel(upper, lower, more_upper, more_lower, smoother, rhs, first):
    quarter = upper.shape[0]
    skip = kept_side() * 2 * quarter
    for total, more, at in ((upper, more_upper, 0), (lower, more_lower, quarter)):
        full = [total[r] + more[r].astype(f32) for r in range(quarter)]
        products = [dot(smoother[skip + at + r], full[r].astype(bf16)) for r in range(quarter)]
        for r in range(quarter):
            rhs[at + r] = full[r]
            first[at + r] = (damping * products[r]).astype(bf16)


def coarse_first(upper, lower, more_upper, more_lower, smoother):
    n, b, k = 2 * upper.shape[0], upper.shape[1], upper.shape[2]
    return pl.pallas_call(
        coarse_first_kernel,
        in_specs=[vmem] * 5,
        out_specs=[vmem] * 2,
        out_shape=[shape(f32, n, b, k), shape(bf16, n, b, k)],
        compiler_params=params(16),
        cost_estimate=cost(2 * n * b * b * k, 12 * n * b * k + 4 * n * b * b),
        name="coarse_first",
    )(upper, lower, more_upper, more_lower, smoother)


def coarse_second_kernel(
    step, cols, halo, own, other, blocks, smoother, rhs, out, extended
):
    n = own.shape[0]
    skip = kept_side() * n
    base = lax.axis_index("rows") * 2 * n + skip - n
    at = 2 * skip
    extended[pl.ds(at, n)] = halo[...]
    extended[n : 2 * n] = own[...]
    extended[pl.ds(2 * n - at, n)] = other[...]

    @pl.loop(0, n // step)
    def _(s):
        image = images(step, s, cols, base, skip, n, blocks, extended)
        rows = [s * step + r for r in range(step)]
        first = [damping * dot(smoother[skip + i], rhs[i].astype(bf16)) for i in rows]
        residual = [(rhs[i] - image[r]).astype(bf16) for r, i in enumerate(rows)]
        products = [dot(smoother[skip + i], residual[r]) for r, i in enumerate(rows)]
        for r, i in enumerate(rows):
            out[i] = first[r] + damping * products[r]


def coarse_second(cols, halo, own, other, blocks, smoother, rhs):
    n, b, k = rhs.shape
    near, step = cols.shape[0], 16
    return pl.pallas_call(
        functools.partial(coarse_second_kernel, step),
        in_specs=[smem] + [vmem] * 6,
        out_specs=vmem,
        out_shape=shape(f32, n, b, k),
        scratch_shapes=[pltpu.VMEM((3 * n, b, k), bf16)],
        compiler_params=params(12),
        cost_estimate=cost(2 * n * b * b * k * (near + 3), 2 * n * b * b * (near + 2) + 14 * n * b * k),
        name="coarse_second",
    )(cols, halo, own, other, blocks, smoother, rhs)


def correct_kernel(aggregate, lower, upper, kept, given, out, staged, sem):
    half, n = kept.shape[0], staged.shape[0]
    turn = kept_side() * half - lax.axis_index("rows") * 2 * half + 2 * half
    copies = []
    for s in range(sem.shape[0]):
        step = n // sem.shape[0]
        for r in range(s * step, (s + 1) * step):
            fine = lower[r] if r < n // 2 else upper[r - n // 2]
            slot = lax.rem(aggregate[r] + turn, 2 * half)
            row = lax.rem(slot, half)
            staged[r] = fine + jnp.where(slot < half, kept[row], given[row])
        rows = slice(s * step, (s + 1) * step)
        copies.append(pltpu.make_async_copy(staged.at[rows], out.at[rows], sem.at[s]))
        copies[-1].start()
    for c in copies:
        c.wait()


def corrected(aggregate, lower, upper, kept, given):
    n, b, k = aggregate.shape[0], lower.shape[1], lower.shape[2]
    return pl.pallas_call(
        correct_kernel,
        in_specs=[smem] + [vmem] * 4,
        out_specs=hbm,
        out_shape=shape(f32, n, b, k),
        scratch_shapes=[
            pltpu.VMEM((n, b, k), f32),
            pltpu.SemaphoreType.DMA((4,)),
        ],
        compiler_params=params(16),
        cost_estimate=cost(n * b * k, 12 * n * b * k),
        name="corrected",
    )(aggregate, lower, upper, kept, given)


def on_device(
    rhs,
    fine_diag,
    fine_smoother,
    fine_blocks,
    fine_cols,
    aggregate,
    coarse_diag,
    coarse_smoother,
    coarse_blocks,
    coarse_cols,
):
    grp, rows = lax.axis_size("grp"), lax.axis_size("rows")
    coarse = coarse_diag.shape[0]
    half = coarse // 2
    fine_cols, coarse_cols = fine_cols.T, coarse_cols.T
    ends = range(grp * rows - 1)
    to_next = lambda v: lax.ppermute(v, fine_axes, [(i, i + 1) for i in ends])
    to_previous = lambda v: lax.ppermute(v, fine_axes, [(i + 1, i) for i in ends])

    high = first_iterate(True, fine_smoother, rhs)
    before = to_next(high)
    low = first_iterate(False, fine_smoother, rhs)
    after = to_previous(low)
    fine = packed(fine_blocks, fine_diag)
    lower, low2 = second_iterate(False, fine_cols, (before, low, high), fine, fine_smoother, rhs)
    after2 = to_previous(low2)
    upper, high2 = second_iterate(True, fine_cols, (low, high, after), fine, fine_smoother, rhs)
    before2 = to_next(high2)
    total = restricted(True, fine_cols, aggregate, (low2, high2, after2), fine, rhs, coarse)
    total = restricted(False, fine_cols, aggregate, (before2, low2, high2), fine, rhs, coarse, total)
    kept, given = total[:half], total[half:]

    across = [(i, i ^ 1) for i in range(grp)]
    near = [(i, i ^ 2) for i in range(grp)]
    far = [(i, i ^ 6) for i in range(grp)]
    total = kept + lax.ppermute(given, "grp", across)
    quarter = half // 2
    one, two = total[:quarter], total[quarter:]
    from_one = lax.ppermute(one.astype(bf16), "grp", near)
    from_two = lax.ppermute(two.astype(bf16), "grp", far)
    one, two = one + from_one.astype(f32), two + from_two.astype(f32)
    from_one = lax.ppermute(one.astype(bf16), "grp", far)
    from_two = lax.ppermute(two.astype(bf16), "grp", near)

    coarse_rhs, rounded_first = coarse_first(one, two, from_one, from_two, coarse_smoother)
    towards = []
    for i in range(grp):
        for r in range(rows):
            source = r - 1 if (i + r) % 2 == 0 else r + 1
            if 0 <= source < rows:
                towards.append((i * rows + source, i * rows + r))
    halo = lax.ppermute(rounded_first, fine_axes, towards)
    own, blocks = lax.optimization_barrier((rounded_first, packed(coarse_blocks, coarse_diag)))
    other = lax.ppermute(own, "grp", across)
    mine = coarse_second(
        coarse_cols,
        halo,
        rounded_first,
        other,
        blocks,
        coarse_smoother,
        coarse_rhs,
    )
    theirs = lax.ppermute(mine, "grp", across)
    return corrected(aggregate, lower, upper, mine, theirs)


def solution(mesh):
    in_specs = (
        P(("grp", "rows"), None, None),
        P(("grp", "rows"), None, None),
        P(("grp", "rows"), None, None),
        P(("grp", "rows"), None, None, None),
        P(("grp", "rows"), None),
        P(("grp", "rows")),
        P("rows", None, None),
        P("rows", None, None),
        P("rows", None, None, None),
        P("rows", None),
    )
    out_specs = P(("grp", "rows"), None, None)
    return jax.shard_map(
        on_device, mesh=mesh, in_specs=in_specs, out_specs=out_specs, check_vma=False
    )
```
